256 devices in a mesh: row: 8 (over z), col: 8 (over y, core), tensor: 4 (over x).
Axes of the slice: x: 4, y: 4, z: 8, core: 2. Of those that a mesh axis runs over, the one named last changes fastest.
Arguments:
- hidden: bfloat16 [3072, 16, 11008], P(('row', 'col'), None, 'tensor'), may hold values from -6 to 6
- cotangent: bfloat16 [3072, 16, 4096], P(('row', 'col'), None, 'tensor'), may hold values from -6 to 6
- tile_live: int32 [64, 2], P(('row', 'col')), may hold values 0 or 1
Outputs:
- ntk_tiles: float32 [64, 2, 48, 48], P(('row', 'col'), None, 'tensor')
The draws below stay inside these ranges and needn't reach their ends.
All inputs are finite; a program needn't handle non-finite values. No bound on the sum of `tile_live` on one device may be relied on, other than what follows from the above.
Results may differ from the reference program's by a relative error of at most 0.0003.
Values may be sent and summed in bfloat16 or wider, within the bound.
A program may use at most 64 MiB of HBM per device.

```python
import math
import jax
import jax.numpy as jnp
from jax import lax

D = 4096
FF = 11008
L = 16
SD = 48
OFFSETS = 2
BLOCKS = 64
N = 3072
N_ROW = 8
N_COL = 8


def touch_ends(entries, rng, least, top_value):
    longest = entries.shape.index(max(entries.shape))
    spots = []
    for shift in (0, 1):
        where = [jax.random.randint(jax.random.fold_in(rng, axis), (), 0, length) for axis, length in enumerate(entries.shape)]
        where[longest] = (where[longest] + shift) % entries.shape[longest]
        spots.append(tuple(where))
    return entries.at[spots[0]].set(least).at[spots[1]].set(top_value)


def levels(own_key, dims, cuts, low, top_value):
    level = 1.0
    for position, shards_of in cuts:
        heights = jax.random.uniform(jax.random.fold_in(jax.random.fold_in(own_key, 6), position), (shards_of,), jnp.float32, low / len(cuts), top_value / len(cuts))
        level = level * jnp.repeat(jnp.exp(heights), dims[position] // shards_of).reshape((-1,) + (1,) * (len(dims) - 1 - position))
    return level


def bell_draw(own_key, dims, deviation, most, shards=(), kind=jnp.bfloat16):
    array = deviation * jax.random.normal(own_key, dims, jnp.float32)
    if shards:
        array = array * levels(own_key, dims, shards, -0.22, 0.18)
    return jnp.clip(array, -most, most).astype(kind)


def setup_inputs(seed: int = 0) -> dict:
    seeds = jax.random.split(jax.random.key(seed), 4)
    return {
        "hidden": bell_draw(seeds[0], (N, L, FF), 1.0, 6.0, ((0, 64), (2, 4))),
        "cotangent": bell_draw(seeds[1], (N, L, D), 1.0, 6.0, ((0, 64), (2, 4))),
        "tile_live": touch_ends((jax.random.randint(seeds[2], (BLOCKS, OFFSETS), 0, 2) < 1).astype(jnp.int32), jax.random.fold_in(seeds[2], 1), 0, 1),
    }


def reference(hidden, cotangent, tile_live):
    block_count = N_ROW * N_COL
    block_rows = SD * L
    hidden_blocks = hidden.reshape(block_count, block_rows, FF)
    cotan_blocks = cotangent.reshape(block_count, block_rows, D)
    kernel_scale = 1.0 / (L * math.sqrt(FF * D))
    live_flags = tile_live.astype(jnp.float32)

    def one_block(device):
        own_hidden = hidden_blocks[device]
        own_cotan = cotan_blocks[device]
        kernel_tiles = []
        for offset_step in range(1, OFFSETS + 1):
            source = (device - offset_step) % block_count
            left_gram = jnp.dot(hidden_blocks[source], own_hidden.T, preferred_element_type=jnp.float32)
            right_gram = jnp.dot(cotan_blocks[source], own_cotan.T, preferred_element_type=jnp.float32)
            product = (left_gram * right_gram).reshape(SD, L, SD, L)
            kernel_tiles.append(lax.optimization_barrier(jnp.sum(product, axis=(1, 3))) * kernel_scale * live_flags[device, offset_step - 1])
        return jnp.stack(kernel_tiles)
    return lax.map(one_block, jnp.arange(block_count, dtype=jnp.int32))
```

```python
import functools
import math

import jax
import jax.numpy as jnp
from jax import lax
from jax.experimental import pallas as pl
from jax.experimental.pallas import tpu as pltpu
from jax.sharding import PartitionSpec as P

D = 4096
FF = 11008
CHUNKS = 6
PARTS = 4
LANES = 128
NEAR, FAR = 0, 1
LEFT, RIGHT = 0, 1


def contract(rows, columns):
    return lax.dot_general(
        rows, columns, (((1,), (1,)), ((), ())), preferred_element_type=jnp.float32
    )


def exact_dot(a, b):
    return jnp.dot(
        a, b, precision=lax.Precision.HIGHEST, preferred_element_type=jnp.float32
    )


def tile_kernel(
    grid_rows,
    grid_cols,
    hidden_ref,
    cotan_ref,
    out_ref,
    own_hidden,
    own_cotan,
    got_hidden,
    got_cotan,
    gram,
    relay_in,
    direct_in,
    passed,
    passed_in,
    row_sums,
    lane_pick,
    keep,
    row_pick,
    result,
    landed,
    load_sem,
    far_send,
    near_send,
    got_sem,
    first_send,
    relay_recv,
    direct_recv,
    pass_send,
    pass_recv,
    result_send,
    result_recv,
):
    row = lax.axis_index("row")
    col = lax.axis_index("col")
    me = lax.axis_index("tensor")
    core = lax.rem(col, 2)
    units = 2 * CHUNKS
    block_rows = own_hidden.shape[0]
    quarter = block_rows // PARTS
    piece = quarter // CHUNKS
    width = hidden_ref.shape[-1]
    cotan_width = cotan_ref.shape[-1]

    up = lax.rem(me + 1, PARTS)
    down = lax.rem(me + PARTS - 1, PARTS)
    across = lax.rem(me + 2, PARTS)
    up_id = (row, col, up)
    down_id = (row, col, down)
    partner_id = (row, col + 1 - 2 * core, me)
    next_id = (
        lax.rem(row + (col + 2) // grid_cols, grid_rows),
        lax.rem(col + 2, grid_cols),
        me,
    )
    prev_id = (
        lax.rem(row + grid_rows - 1 + (col + grid_cols - 2) // grid_cols, grid_rows),
        lax.rem(col + grid_cols - 2, grid_cols),
        me,
    )
    even = core == 0
    far_id = tuple(jnp.where(even, p, n) for p, n in zip(prev_id, next_id))

    loads = (
        pltpu.make_async_copy(hidden_ref, own_hidden_view(own_hidden, piece), load_sem.at[0]),
        pltpu.make_async_copy(cotan_ref, own_hidden_view(own_cotan, piece), load_sem.at[1]),
    )
    for load in loads:
        load.start()

    barrier = pltpu.get_barrier_semaphore()
    peers = (up_id, down_id, partner_id, next_id, prev_id)
    for peer in peers:
        pl.semaphore_signal(
            barrier, inc=1, device_id=peer, device_id_type=pl.DeviceIdType.MESH
        )
    pl.semaphore_wait(barrier, len(peers))

    def send(source, target, send_sem, recv_sem, device):
        return pltpu.make_async_remote_copy(
            src_ref=source,
            dst_ref=target,
            send_sem=send_sem,
            recv_sem=recv_sem,
            device_id=device,
            device_id_type=pl.DeviceIdType.MESH,
        )

    def far_copies(k):
        slot = FAR * CHUNKS + k
        return (
            send(hidden_ref.at[:, k], got_hidden.at[slot], far_send.at[k, 0], got_sem.at[slot, 0], far_id),
            send(cotan_ref.at[:, k], got_cotan.at[slot], far_send.at[k, 1], got_sem.at[slot, 1], far_id),
        )

    def near_copies_own(k):
        return (
            send(hidden_ref.at[:, k], got_hidden.at[k], near_send.at[k, 0], got_sem.at[k, 0], partner_id),
            send(cotan_ref.at[:, k], got_cotan.at[k], near_send.at[k, 1], got_sem.at[k, 1], partner_id),
        )

    def near_copies_on(k):
        slot = FAR * CHUNKS + k
        return (
            send(got_hidden.at[slot], got_hidden.at[k], near_send.at[k, 0], got_sem.at[k, 0], partner_id),
            send(got_cotan.at[slot], got_cotan.at[k], near_send.at[k, 1], got_sem.at[k, 1], partner_id),
        )

    @pl.loop(0, CHUNKS)
    def _(k):
        for copy in far_copies(k):
            copy.start()

        @pl.when(even)
        def _():
            for copy in near_copies_own(k):
                copy.start()

    def unit_of(n):
        lead = CHUNKS // 2
        later = n - lead
        even_stream = jnp.where(lax.rem(n, 2) == 0, FAR, NEAR)
        mixed = lax.rem(later, 2) == 0
        odd_stream = jnp.where(
            n < lead, NEAR, jnp.where(later < CHUNKS, jnp.where(mixed, FAR, NEAR), FAR)
        )
        odd_chunk = jnp.where(
            n < lead,
            n,
            jnp.where(
                later < CHUNKS,
                jnp.where(mixed, later // 2, lead + later // 2),
                later - lead,
            ),
        )
        return (
            jnp.where(even, even_stream, odd_stream),
            jnp.where(even, n // 2, odd_chunk),
        )

    def relayed_after(n):
        lead = CHUNKS // 2
        paired = jnp.where(lax.rem(n, 2) == 0, n, n + 1)
        crossed = jnp.where(lax.rem(n, 2) == 0, n + 1, n)
        odd_count = jnp.where(
            n < lead, n, jnp.where(n < lead + CHUNKS, crossed, n + 1)
        )
        return jnp.where(even, paired, odd_count)

    def first_copies(n):
        return (
            send(gram.at[n, LEFT, across], relay_in.at[n, LEFT], first_send.at[n, 0], relay_recv.at[n, LEFT], up_id),
            send(gram.at[n, RIGHT, across], relay_in.at[n, RIGHT], first_send.at[n, 1], relay_recv.at[n, RIGHT], down_id),
            send(gram.at[n, RIGHT, up], direct_in.at[n, RIGHT], first_send.at[n, 2], direct_recv.at[n, RIGHT], up_id),
            send(gram.at[n, LEFT, down], direct_in.at[n, LEFT], first_send.at[n, 3], direct_recv.at[n, LEFT], down_id),
        )

    def pass_copies(n):
        return (
            send(passed.at[n, LEFT], passed_in.at[n, LEFT], pass_send.at[n, LEFT], pass_recv.at[n, LEFT], up_id),
            send(passed.at[n, RIGHT], passed_in.at[n, RIGHT], pass_send.at[n, RIGHT], pass_recv.at[n, RIGHT], down_id),
        )

    def compute(n, stream, k):
        slot = stream * CHUNKS + k
        natural = jnp.logical_and(even, stream == FAR)

        def grams(own, got, which):
            chunk = got[slot].reshape(PARTS * piece, got.shape[-1])

            @pl.when(natural)
            def _():
                for part in range(PARTS):
                    gram[n, which, part] = contract(
                        own[part * quarter : (part + 1) * quarter, :], chunk
                    )

            @pl.when(jnp.logical_not(natural))
            def _():
                wide = 2 * LANES
                for block in range(block_rows // wide):
                    value = contract(chunk, own[block * wide : (block + 1) * wide, :])
                    for part in range(PARTS):
                        for half in range(2):
                            start = (2 * block + half) * piece
                            gram[n, which, part, start : start + piece, :] = value[
                                part * piece : (part + 1) * piece,
                                half * LANES : (half + 1) * LANES,
                            ]

        grams(own_hidden, got_hidden, LEFT)
        grams(own_cotan, got_cotan, RIGHT)

    def relay(n):
        copies, onward = first_copies(n), pass_copies(n)
        copies[0].wait_recv()
        passed[n, LEFT] = relay_in[n, LEFT] + gram[n, LEFT, up]
        onward[0].start()
        copies[1].wait_recv()
        passed[n, RIGHT] = relay_in[n, RIGHT] + gram[n, RIGHT, down]
        onward[1].start()

    def finish(n):
        stream, k = unit_of(n)
        copies, onward = first_copies(n), pass_copies(n)
        copies[2].wait_recv()
        copies[3].wait_recv()
        onward[0].wait_recv()
        onward[1].wait_recv()
        left = gram[n, LEFT, me] + passed_in[n, LEFT] + direct_in[n, LEFT]
        right = gram[n, RIGHT, me] + passed_in[n, RIGHT] + direct_in[n, RIGHT]
        product = left * right
        tokens = 16
        row_sums[stream * CHUNKS + k, : quarter // tokens, :] = jnp.sum(
            product.reshape(quarter // tokens, tokens, LANES), axis=1
        )

    row_sums[...] = jnp.zeros_like(row_sums)
    build_picks(even, lane_pick, keep, row_pick)
    for load in loads:
        load.wait()

    @pl.loop(0, units)
    def _(n):
        stream, k = unit_of(n)
        slot = stream * CHUNKS + k
        send(hidden_ref.at[:, k], got_hidden.at[slot], far_send.at[k, 0], got_sem.at[slot, 0], far_id).wait_recv()
        send(cotan_ref.at[:, k], got_cotan.at[slot], far_send.at[k, 1], got_sem.at[slot, 1], far_id).wait_recv()

        @pl.when(jnp.logical_and(jnp.logical_not(even), stream == FAR))
        def _():
            for copy in near_copies_on(k):
                copy.start()

        compute(n, stream, k)
        for copy in first_copies(n):
            copy.start()

        @pl.loop(jnp.where(n > 0, relayed_after(n - 1), 0), relayed_after(n))
        def _(m):
            relay(m)

        @pl.when(n >= 2)
        def _():
            finish(n - 2)

    def epilogue(stream):
        sums = row_sums[pl.ds(stream * CHUNKS, CHUNKS)].reshape(CHUNKS * 16, LANES)
        spread = exact_dot(sums, lane_pick[stream]) * keep[stream]
        result[stream] = exact_dot(row_pick[stream], spread)

    result_copy = send(result.at[FAR], landed, result_send, result_recv, next_id)
    finish(units - 2)
    epilogue(jnp.where(even, FAR, NEAR))

    @pl.when(even)
    def _():
        result_copy.start()

    finish(units - 1)
    epilogue(jnp.where(even, NEAR, FAR))
    out_ref[0] = result[NEAR]

    @pl.when(even)
    def _():
        result_copy.wait()
        out_ref[1] = landed[...]

    @pl.when(jnp.logical_not(even))
    def _():
        out_ref[1] = result[FAR]

    @pl.loop(0, CHUNKS)
    def _(k):
        for copy in far_copies(k):
            copy.wait_send()
        for copy in near_copies_own(k):
            copy.wait_send()

    @pl.loop(0, units)
    def _(n):
        for copy in first_copies(n):
            copy.wait_send()
        for copy in pass_copies(n):
            copy.wait_send()


def own_hidden_view(own, piece):
    return own.reshape(PARTS, CHUNKS, piece, own.shape[-1])


def build_picks(even, lane_pick, keep, row_pick):
    def iota(shape, axis):
        return lax.broadcasted_iota(jnp.int32, shape, axis)

    def twelfth(j):
        return (
            (j >= 12).astype(jnp.int32)
            + (j >= 24).astype(jnp.int32)
            + (j >= 36).astype(jnp.int32)
        )

    held = CHUNKS * 16
    lane, target = iota((LANES, LANES), 0), iota((LANES, LANES), 1)
    group = lane >> 4
    own = jnp.logical_and(group == (target & 7), target < 48).astype(jnp.float32)
    other = jnp.logical_and(
        group == 2 * twelfth(target) + (target & 1), target < 48
    ).astype(jnp.float32)
    line, target = iota((held, LANES), 0), iota((held, LANES), 1)
    own_keep = (((line & 15) >> 1) == (target >> 3)).astype(jnp.float32)
    other_keep = (
        (line >> 4) == ((target - 12 * twelfth(target)) >> 1)
    ).astype(jnp.float32)
    out, line = iota((16, held), 0), iota((16, held), 1)
    place = line & 15
    own_row = jnp.logical_and(
        2 * (line >> 4) + (place & 1) == out, place < 12
    ).astype(jnp.float32)
    other_row = jnp.logical_and(place == out, place < 12).astype(jnp.float32)
    lane_pick[NEAR] = own
    keep[NEAR] = own_keep
    row_pick[NEAR] = own_row
    lane_pick[FAR] = jnp.where(even, other, own)
    keep[FAR] = jnp.where(even, other_keep, own_keep)
    row_pick[FAR] = jnp.where(even, other_row, own_row)


def solution(mesh):
    grid_rows, grid_cols = mesh.shape["row"], mesh.shape["col"]
    placed = (
        P(("row", "col"), None, "tensor"),
        P(("row", "col"), None, "tensor"),
        P(("row", "col"), None),
    )

    def per_device(hidden, cotangent, tile_live):
        samples, tokens, width = hidden.shape
        cotan_width = cotangent.shape[2]
        block_rows = samples * tokens
        quarter = block_rows // PARTS
        piece = quarter // CHUNKS
        units = 2 * CHUNKS
        f32, bf16 = jnp.float32, jnp.bfloat16
        vmem, dma = pltpu.VMEM, pltpu.SemaphoreType.DMA
        held = pltpu.MemorySpace.HBM
        part = (quarter, LANES)
        sums = pl.pallas_call(
            functools.partial(tile_kernel, grid_rows, grid_cols),
            out_shape=jax.ShapeDtypeStruct((2, 16, LANES), f32),
            in_specs=[pl.BlockSpec(memory_space=held)] * 2,
            out_specs=pl.BlockSpec(memory_space=pltpu.VMEM),
            scratch_shapes=[
                vmem((block_rows, width), bf16),
                vmem((block_rows, cotan_width), bf16),
                vmem((units, PARTS, piece, width), bf16),
                vmem((units, PARTS, piece, cotan_width), bf16),
                vmem((units, 2, PARTS) + part, f32),
                vmem((units, 2) + part, f32),
                vmem((units, 2) + part, f32),
                vmem((units, 2) + part, f32),
                vmem((units, 2) + part, f32),
                vmem((units, 16, LANES), f32),
                vmem((2, LANES, LANES), f32),
                vmem((2, CHUNKS * 16, LANES), f32),
                vmem((2, 16, CHUNKS * 16), f32),
                vmem((2, 16, LANES), f32),
                vmem((16, LANES), f32),
                dma((2,)),
                dma((CHUNKS, 2)),
                dma((CHUNKS, 2)),
                dma((units, 2)),
                dma((units, 4)),
                dma((units, 2)),
                dma((units, 2)),
                dma((units, 2)),
                dma((units, 2)),
                dma,
                dma,
            ],
            compiler_params=pltpu.CompilerParams(
                collective_id=0,
                has_side_effects=True,
                vmem_limit_bytes=60 * 1024 * 1024,
            ),
        )(
            hidden.reshape(PARTS, CHUNKS, piece, width),
            cotangent.reshape(PARTS, CHUNKS, piece, cotan_width),
        )
        kernel_scale = 1.0 / (tokens * math.sqrt(FF * D))
        live = tile_live[0].astype(f32)[:, None, None] * kernel_scale
        return (sums[:, : samples // PARTS, :samples] * live)[None]

    return jax.shard_map(
        per_device,
        mesh=mesh,
        in_specs=placed,
        out_specs=P(("row", "col"), None, "tensor", None),
        check_vma=False,
    )
```

```python
import functools
import math

import jax
import jax.numpy as jnp
from jax import lax
from jax.experimental import pallas as pl
from jax.experimental.pallas import tpu as pltpu
from jax.sharding import PartitionSpec as P

D = 4096
FF = 11008
CHUNKS = 6
PARTS = 4
LANES = 128
TOKENS = 16
NEAR, FAR = 0, 1
UP, DOWN = 0, 1
STEPS = 127.0 * 256.0
LEFT, RIGHT = 0, 1


def contract(rows, columns):
    return lax.dot_general(
        rows, columns, (((1,), (1,)), ((), ())), preferred_element_type=jnp.float32
    )


def exact_dot(a, b):
    return jnp.dot(
        a, b, precision=lax.Precision.HIGHEST, preferred_element_type=jnp.float32
    )


def pack(value, head_ref, rest_ref):
    half = value.shape[0] // 2
    head = value.astype(jnp.bfloat16)
    wide = head.astype(jnp.float32)
    rest = jnp.round((value - wide) * (STEPS / jnp.maximum(jnp.abs(wide), 1e-30)))
    both = rest[:half] * 256.0 + rest[half:]
    head_ref[...] = head
    rest_ref[...] = both.astype(jnp.int32).astype(jnp.int16)


def unpack(head_ref, rest_ref):
    wide = head_ref[...].astype(jnp.float32)
    both = rest_ref[...].astype(jnp.int32).astype(jnp.float32)
    first = jnp.floor((both + 128.0) * (1.0 / 256.0))
    rest = jnp.concatenate([first, both - 256.0 * first], axis=0)
    return wide + jnp.abs(wide) * (rest * (1.0 / STEPS))


def tile_kernel(
    grid_rows,
    grid_cols,
    hidden_ref,
    cotan_ref,
    out_ref,
    own_hidden,
    own_cotan,
    got_hidden,
    got_cotan,
    gram,
    first_head,
    first_rest,
    first_head_in,
    first_rest_in,
    pass_head,
    pass_rest,
    pass_head_in,
    pass_rest_in,
    row_sums,
    lane_pick,
    keep,
    row_pick,
    result,
    landed,
    load_sem,
    block_send,
    got_sem,
    first_send,
    first_recv,
    pass_send,
    pass_recv,
    result_send,
    result_recv,
):
    row = lax.axis_index("row")
    col = lax.axis_index("col")
    me = lax.axis_index("tensor")
    core = lax.rem(col, 2)
    even = core == 0
    odd = core == 1
    units = 2 * CHUNKS
    block_rows = own_hidden.shape[0]
    quarter = block_rows // PARTS
    piece = quarter // CHUNKS

    up = lax.rem(me + 1, PARTS)
    down = lax.rem(me + PARTS - 1, PARTS)
    across = lax.rem(me + 2, PARTS)
    up_id = (row, col, up)
    down_id = (row, col, down)
    partner_id = (row, col + 1 - 2 * core, me)
    next_id = (
        lax.rem(row + (col + 2) // grid_cols, grid_rows),
        lax.rem(col + 2, grid_cols),
        me,
    )
    prev_id = (
        lax.rem(row + grid_rows - 1 + (col + grid_cols - 2) // grid_cols, grid_rows),
        lax.rem(col + grid_cols - 2, grid_cols),
        me,
    )
    far_id = tuple(jnp.where(even, p, n) for p, n in zip(prev_id, next_id))

    def by_piece(own):
        return own.reshape(PARTS, CHUNKS, piece, own.shape[-1])

    loads = (
        pltpu.make_async_copy(hidden_ref, by_piece(own_hidden), load_sem.at[0]),
        pltpu.make_async_copy(cotan_ref, by_piece(own_cotan), load_sem.at[1]),
    )
    for load in loads:
        load.start()

    barrier = pltpu.get_barrier_semaphore()
    peers = (up_id, down_id, partner_id, next_id, prev_id)
    for peer in peers:
        pl.semaphore_signal(
            barrier, inc=1, device_id=peer, device_id_type=pl.DeviceIdType.MESH
        )
    pl.semaphore_wait(barrier, len(peers))

    def send(source, target, send_sem, recv_sem, device):
        return pltpu.make_async_remote_copy(
            src_ref=source,
            dst_ref=target,
            send_sem=send_sem,
            recv_sem=recv_sem,
            device_id=device,
            device_id_type=pl.DeviceIdType.MESH,
        )

    def block_copies(stream, k, device):
        return tuple(
            send(
                source.at[:, k],
                target.at[stream, :, k],
                block_send.at[stream, k, which],
                got_sem.at[stream, k, which],
                device,
            )
            for which, (source, target) in enumerate(
                ((hidden_ref, got_hidden), (cotan_ref, got_cotan))
            )
        )

    @pl.loop(0, CHUNKS)
    def _(k):
        for copy in block_copies(FAR, k, far_id):
            copy.start()
        for copy in block_copies(NEAR, k, partner_id):
            copy.start()

    def wait_block(stream, k):
        for copy in block_copies(stream, k, partner_id):
            copy.wait_recv()

    def unit_of(n):
        return (
            jnp.where(even, n // CHUNKS, lax.rem(n, 2)),
            jnp.where(even, lax.rem(n, CHUNKS), n // 2),
        )

    def relayed_after(n):
        late = jnp.where(n < CHUNKS + 2, n, n + 1)
        paired = jnp.where(lax.rem(n, 2) == 0, n, n + 1)
        return jnp.where(even, late, paired)

    def first_copies(n, way):
        device = (up_id, down_id)[way]
        return (
            send(first_head.at[n, way], first_head_in.at[n, way], first_send.at[n, way, 0], first_recv.at[n, way, 0], device),
            send(first_rest.at[n, way], first_rest_in.at[n, way], first_send.at[n, way, 1], first_recv.at[n, way, 1], device),
        )

    def pass_copies(n, way):
        device = (up_id, down_id)[way]
        return (
            send(pass_head.at[n, way], pass_head_in.at[n, way], pass_send.at[n, way, 0], pass_recv.at[n, way, 0], device),
            send(pass_rest.at[n, way], pass_rest_in.at[n, way], pass_send.at[n, way, 1], pass_recv.at[n, way, 1], device),
        )

    def rows_first(n, which, own, chunk):
        wide = 2 * LANES
        for block in range(block_rows // wide):
            value = contract(chunk, own[block * wide : (block + 1) * wide, :])
            for part in range(PARTS):
                for half in range(2):
                    start = (2 * block + half) * piece
                    gram[n, which, part, start : start + piece, :] = value[
                        part * piece : (part + 1) * piece,
                        half * LANES : (half + 1) * LANES,
                    ]

    def compute(n, tile, k):
        def chunk_of(got, stream):
            return got[stream, :, k].reshape(PARTS * piece, got.shape[-1])

        pairs = ((own_hidden, got_hidden), (own_cotan, got_cotan))

        @pl.when(even)
        def _():
            for which, (own, got) in enumerate(pairs):
                chunk = chunk_of(got, tile)
                for part in range(PARTS):
                    gram[n, which, part] = contract(
                        own[part * quarter : (part + 1) * quarter, :], chunk
                    )

        @pl.when(jnp.logical_and(odd, tile == 0))
        def _():
            for which, (_, got) in enumerate(pairs):
                other = got.at[NEAR].reshape(block_rows, got.shape[-1])
                rows_first(n, which, other, chunk_of(got, FAR))

        @pl.when(jnp.logical_and(odd, tile == 1))
        def _():
            for which, (own, got) in enumerate(pairs):
                rows_first(n, which, own, chunk_of(got, FAR))

        pack(gram[n, LEFT, across], first_head.at[n, UP, 0], first_rest.at[n, UP, 0])
        pack(gram[n, RIGHT, up], first_head.at[n, UP, 1], first_rest.at[n, UP, 1])
        pack(gram[n, RIGHT, across], first_head.at[n, DOWN, 0], first_rest.at[n, DOWN, 0])
        pack(gram[n, LEFT, down], first_head.at[n, DOWN, 1], first_rest.at[n, DOWN, 1])
        for way in (UP, DOWN):
            for copy in first_copies(n, way):
                copy.start()

    def relay(n):
        for way, which, onward in ((UP, LEFT, up), (DOWN, RIGHT, down)):
            for copy in first_copies(n, way):
                copy.wait_recv()
            total = gram[n, which, onward] + unpack(
                first_head_in.at[n, way, 0], first_rest_in.at[n, way, 0]
            )
            pack(total, pass_head.at[n, way], pass_rest.at[n, way])
            for copy in pass_copies(n, way):
                copy.start()

    def finish(n):
        tile, k = unit_of(n)
        for way in (UP, DOWN):
            for copy in pass_copies(n, way):
                copy.wait_recv()
        left, right = (
            gram[n, which, me]
            + unpack(pass_head_in.at[n, way], pass_rest_in.at[n, way])
            + unpack(first_head_in.at[n, 1 - way, 1], first_rest_in.at[n, 1 - way, 1])
            for which, way in ((LEFT, UP), (RIGHT, DOWN))
        )
        row_sums[tile * CHUNKS + k, : quarter // TOKENS, :] = jnp.sum(
            (left * right).reshape(quarter // TOKENS, TOKENS, LANES), axis=1
        )

    def epilogue(tile):
        sums = row_sums[pl.ds(tile * CHUNKS, CHUNKS)].reshape(CHUNKS * TOKENS, LANES)
        result[tile] = exact_dot(row_pick[...], exact_dot(sums, lane_pick[...]) * keep[...])

    swapped = send(result.at[0], landed.at[0], result_send.at[0], result_recv.at[0], partner_id)
    moved = send(result.at[1], landed.at[1], result_send.at[1], result_recv.at[1], next_id)

    row_sums[...] = jnp.zeros_like(row_sums)
    build_picks(even, lane_pick, keep, row_pick)
    for load in loads:
        load.wait()

    @pl.when(odd)
    def _():
        @pl.loop(0, CHUNKS)
        def _(k):
            wait_block(NEAR, k)

    @pl.loop(0, units)
    def _(n):
        tile, k = unit_of(n)

        @pl.when(jnp.logical_or(even, tile == 0))
        def _():
            wait_block(jnp.where(even, tile, FAR), k)

        compute(n, tile, k)

        @pl.loop(jnp.where(n > 0, relayed_after(n - 1), 0), relayed_after(n))
        def _(m):
            relay(m)

        @pl.when(n >= 2)
        def _():
            finish(n - 2)

        @pl.when(jnp.logical_and(even, n == CHUNKS + 2))
        def _():
            epilogue(0)
            swapped.start()

    finish(units - 2)

    @pl.when(odd)
    def _():
        epilogue(0)
        swapped.start()

    finish(units - 1)
    epilogue(1)

    @pl.when(even)
    def _():
        moved.start()

    @pl.loop(0, CHUNKS)
    def _(k):
        for stream in (NEAR, FAR):
            for copy in block_copies(stream, k, partner_id):
                copy.wait_send()

    @pl.loop(0, units)
    def _(n):
        for way in (UP, DOWN):
            for copy in first_copies(n, way):
                copy.wait_send()
            for copy in pass_copies(n, way):
                copy.wait_send()

    swapped.wait()
    out_ref[0] = landed[0]

    @pl.when(even)
    def _():
        moved.wait()
        out_ref[1] = landed[1]

    @pl.when(odd)
    def _():
        out_ref[1] = result[1]


def build_picks(even, lane_pick, keep, row_pick):
    def iota(shape, axis):
        return lax.broadcasted_iota(jnp.int32, shape, axis)

    def twelfth(j):
        return (
            (j >= 12).astype(jnp.int32)
            + (j >= 24).astype(jnp.int32)
            + (j >= 36).astype(jnp.int32)
        )

    held = CHUNKS * TOKENS
    lane, target = iota((LANES, LANES), 0), iota((LANES, LANES), 1)
    group = lane >> 4
    by_rows = jnp.logical_and(group == (target & 7), target < 48).astype(jnp.float32)
    by_lanes = jnp.logical_and(
        group == 2 * twelfth(target) + (target & 1), target < 48
    ).astype(jnp.float32)
    lane_pick[...] = jnp.where(even, by_lanes, by_rows)
    line, target = iota((held, LANES), 0), iota((held, LANES), 1)
    by_rows = (((line & 15) >> 1) == (target >> 3)).astype(jnp.float32)
    by_lanes = (
        (line >> 4) == ((target - 12 * twelfth(target)) >> 1)
    ).astype(jnp.float32)
    keep[...] = jnp.where(even, by_lanes, by_rows)
    out, line = iota((16, held), 0), iota((16, held), 1)
    place = line & 15
    by_rows = jnp.logical_and(
        2 * (line >> 4) + (place & 1) == out, place < 12
    ).astype(jnp.float32)
    by_lanes = jnp.logical_and(place == out, place < 12).astype(jnp.float32)
    row_pick[...] = jnp.where(even, by_lanes, by_rows)


def solution(mesh):
    grid_rows, grid_cols = mesh.shape["row"], mesh.shape["col"]
    placed = (
        P(("row", "col"), None, "tensor"),
        P(("row", "col"), None, "tensor"),
        P(("row", "col"), None),
    )

    def per_device(hidden, cotangent, tile_live):
        samples, tokens, width = hidden.shape
        cotan_width = cotangent.shape[2]
        block_rows = samples * tokens
        quarter = block_rows // PARTS
        piece = quarter // CHUNKS
        units = 2 * CHUNKS
        f32, bf16, i16 = jnp.float32, jnp.bfloat16, jnp.int16
        vmem, dma = pltpu.VMEM, pltpu.SemaphoreType.DMA
        held = pltpu.MemorySpace.HBM
        sums = pl.pallas_call(
            functools.partial(tile_kernel, grid_rows, grid_cols),
            out_shape=jax.ShapeDtypeStruct((2, 16, LANES), f32),
            in_specs=[pl.BlockSpec(memory_space=held)] * 2,
            out_specs=pl.BlockSpec(memory_space=pltpu.VMEM),
            scratch_shapes=[
                vmem((block_rows, width), bf16),
                vmem((block_rows, cotan_width), bf16),
                vmem((2, PARTS, CHUNKS, piece, width), bf16),
                vmem((2, PARTS, CHUNKS, piece, cotan_width), bf16),
                vmem((units, 2, PARTS, quarter, LANES), f32),
                vmem((units, 2, 2, quarter, LANES), bf16),
                vmem((units, 2, 2, quarter // 2, LANES), i16),
                vmem((units, 2, 2, quarter, LANES), bf16),
                vmem((units, 2, 2, quarter // 2, LANES), i16),
                vmem((units, 2, quarter, LANES), bf16),
                vmem((units, 2, quarter // 2, LANES), i16),
                vmem((units, 2, quarter, LANES), bf16),
                vmem((units, 2, quarter // 2, LANES), i16),
                vmem((units, TOKENS, LANES), f32),
                vmem((LANES, LANES), f32),
                vmem((CHUNKS * TOKENS, LANES), f32),
                vmem((TOKENS, CHUNKS * TOKENS), f32),
                vmem((2, TOKENS, LANES), f32),
                vmem((2, TOKENS, LANES), f32),
                dma((2,)),
                dma((2, CHUNKS, 2)),
                dma((2, CHUNKS, 2)),
                dma((units, 2, 2)),
                dma((units, 2, 2)),
                dma((units, 2, 2)),
                dma((units, 2, 2)),
                dma((2,)),
                dma((2,)),
            ],
            compiler_params=pltpu.CompilerParams(
                collective_id=0,
                has_side_effects=True,
                vmem_limit_bytes=60 * 1024 * 1024,
            ),
        )(
            hidden.reshape(PARTS, CHUNKS, piece, width),
            cotangent.reshape(PARTS, CHUNKS, piece, cotan_width),
        )
        kernel_scale = 1.0 / (tokens * math.sqrt(FF * D))
        live = tile_live[0].astype(f32)[:, None, None] * kernel_scale
        return (sums[:, : samples // PARTS, :samples] * live)[None]

    return jax.shard_map(
        per_device,
        mesh=mesh,
        in_specs=placed,
        out_specs=P(("row", "col"), None, "tensor", None),
        check_vma=False,
    )
```

```python
import functools
import math

import jax
import jax.numpy as jnp
from jax import lax
from jax.experimental import pallas as pl
from jax.experimental.pallas import tpu as pltpu
from jax.sharding import PartitionSpec as P

D = 4096
FF = 11008
CHUNKS = 6
PARTS = 4
LANES = 128
TOKENS = 16
NEAR, FAR = 0, 1
RELAY, DIRECT = 0, 1
STEPS = 127.0 * 256.0
LEFT, RIGHT = 0, 1


def contract(rows, columns):
    return lax.dot_general(
        rows, columns, (((1,), (1,)), ((), ())), preferred_element_type=jnp.float32
    )


def exact_dot(a, b):
    return jnp.dot(
        a, b, precision=lax.Precision.HIGHEST, preferred_element_type=jnp.float32
    )


def pack(value, head_ref, rest_ref):
    half = value.shape[0] // 2
    head = value.astype(jnp.bfloat16)
    wide = head.astype(jnp.float32)
    rest = jnp.round((value - wide) * (STEPS / jnp.maximum(jnp.abs(wide), 1e-30)))
    both = rest[:half] * 256.0 + rest[half:]
    head_ref[...] = head
    rest_ref[...] = both.astype(jnp.int32).astype(jnp.int16)


def unpack(head_ref, rest_ref):
    wide = head_ref[...].astype(jnp.float32)
    both = rest_ref[...].astype(jnp.int32).astype(jnp.float32)
    first = jnp.floor((both + 128.0) * (1.0 / 256.0))
    rest = jnp.concatenate([first, both - 256.0 * first], axis=0)
    return wide + jnp.abs(wide) * (rest * (1.0 / STEPS))


def tile_kernel(
    grid_rows,
    grid_cols,
    hidden_ref,
    cotan_ref,
    out_ref,
    own_hidden,
    own_cotan,
    got_hidden,
    got_cotan,
    gram,
    first_head,
    first_rest,
    first_head_in,
    first_rest_in,
    pass_head,
    pass_rest,
    pass_head_in,
    pass_rest_in,
    row_sums,
    lane_pick,
    keep,
    row_pick,
    result,
    landed,
    load_sem,
    block_send,
    got_sem,
    first_send,
    first_recv,
    pass_send,
    pass_recv,
    result_send,
    result_recv,
):
    row = lax.axis_index("row")
    col = lax.axis_index("col")
    me = lax.axis_index("tensor")
    core = lax.rem(col, 2)
    even = core == 0
    odd = core == 1
    units = 2 * CHUNKS
    block_rows = own_hidden.shape[0]
    quarter = block_rows // PARTS
    piece = quarter // CHUNKS

    up = lax.rem(me + 1, PARTS)
    down = lax.rem(me + PARTS - 1, PARTS)
    across = lax.rem(me + 2, PARTS)
    up_id = (row, col, up)
    down_id = (row, col, down)
    across_id = (row, col, across)
    partner_id = (row, col + 1 - 2 * core, me)
    next_id = (
        lax.rem(row + (col + 2) // grid_cols, grid_rows),
        lax.rem(col + 2, grid_cols),
        me,
    )
    prev_id = (
        lax.rem(row + grid_rows - 1 + (col + grid_cols - 2) // grid_cols, grid_rows),
        lax.rem(col + grid_cols - 2, grid_cols),
        me,
    )
    far_id = tuple(jnp.where(even, p, n) for p, n in zip(prev_id, next_id))

    def by_piece(own):
        return own.reshape(PARTS, CHUNKS, piece, own.shape[-1])

    loads = (
        pltpu.make_async_copy(hidden_ref, by_piece(own_hidden), load_sem.at[0]),
        pltpu.make_async_copy(cotan_ref, by_piece(own_cotan), load_sem.at[1]),
    )
    for load in loads:
        load.start()

    barrier = pltpu.get_barrier_semaphore()
    peers = (up_id, down_id, across_id, partner_id, next_id, prev_id)
    for peer in peers:
        pl.semaphore_signal(
            barrier, inc=1, device_id=peer, device_id_type=pl.DeviceIdType.MESH
        )
    pl.semaphore_wait(barrier, len(peers))

    def send(source, target, send_sem, recv_sem, device):
        return pltpu.make_async_remote_copy(
            src_ref=source,
            dst_ref=target,
            send_sem=send_sem,
            recv_sem=recv_sem,
            device_id=device,
            device_id_type=pl.DeviceIdType.MESH,
        )

    def block_copy(stream, k, which, device):
        source, target = ((hidden_ref, got_hidden), (cotan_ref, got_cotan))[which]
        return send(
            source.at[:, k],
            target.at[stream, :, k],
            block_send.at[stream, k, which],
            got_sem.at[stream, k, which],
            device,
        )

    @pl.loop(0, CHUNKS)
    def _(k):
        for which in (LEFT, RIGHT):
            block_copy(FAR, k, which, far_id).start()
        for which in (LEFT, RIGHT):
            block_copy(NEAR, k, which, partner_id).start()

    def wait_block(stream, k, which):
        block_copy(stream, k, which, partner_id).wait_recv()

    ways = ((up, up_id, down, down_id), (down, down_id, up, up_id))

    def first_copies(u, which, kind):
        device = ways[which][1 + 2 * kind]
        return (
            send(first_head.at[u, which, kind], first_head_in.at[u, which, kind], first_send.at[u, which, kind, 0], first_recv.at[u, which, kind, 0], device),
            send(first_rest.at[u, which, kind], first_rest_in.at[u, which, kind], first_send.at[u, which, kind, 1], first_recv.at[u, which, kind, 1], device),
        )

    def pass_copies(u, which, straight=False):
        device = across_id if straight else ways[which][1]
        return (
            send(pass_head.at[u, which], pass_head_in.at[u, which], pass_send.at[u, which, 0], pass_recv.at[u, which, 0], device),
            send(pass_rest.at[u, which], pass_rest_in.at[u, which], pass_send.at[u, which, 1], pass_recv.at[u, which, 1], device),
        )

    own = (own_hidden, own_cotan)
    got = (got_hidden, got_cotan)

    def chunk_of(stream, k, which):
        return got[which][stream, :, k].reshape(PARTS * piece, got[which].shape[-1])

    def lanes_first(u, which, rows, chunk):
        for part in range(PARTS):
            gram[u, which, part] = contract(
                rows[part * quarter : (part + 1) * quarter, :], chunk
            )

    def rows_first(u, which, columns, chunk):
        wide = 2 * LANES
        for block in range(block_rows // wide):
            value = contract(chunk, columns[block * wide : (block + 1) * wide, :])
            for part in range(PARTS):
                for half in range(2):
                    start = (2 * block + half) * piece
                    gram[u, which, part, start : start + piece, :] = value[
                        part * piece : (part + 1) * piece,
                        half * LANES : (half + 1) * LANES,
                    ]

    def hand_on(u, which, straight=False):
        if straight:
            pack(gram[u, which, across], pass_head.at[u, which], pass_rest.at[u, which])
            for copy in pass_copies(u, which, straight):
                copy.start()
        relayed = ways[which][0] if straight else across
        for kind, part in ((RELAY, relayed), (DIRECT, ways[which][2])):
            pack(
                gram[u, which, part],
                first_head.at[u, which, kind],
                first_rest.at[u, which, kind],
            )
            for copy in first_copies(u, which, kind):
                copy.start()

    def relay(u, which):
        for copy in first_copies(u, which, RELAY):
            copy.wait_recv()
        total = gram[u, which, ways[which][0]] + unpack(
            first_head_in.at[u, which, RELAY], first_rest_in.at[u, which, RELAY]
        )
        pack(total, pass_head.at[u, which], pass_rest.at[u, which])
        for copy in pass_copies(u, which):
            copy.start()

    def whole(u, which, straight=False):
        for copy in first_copies(u, which, DIRECT):
            copy.wait_recv()
        direct = unpack(
            first_head_in.at[u, which, DIRECT], first_rest_in.at[u, which, DIRECT]
        )
        mine = gram[u, which, me] + direct
        if straight:
            for copy in first_copies(u, which, RELAY):
                copy.wait_recv()
            mine = mine + unpack(
                first_head_in.at[u, which, RELAY], first_rest_in.at[u, which, RELAY]
            )
        for copy in pass_copies(u, which):
            copy.wait_recv()
        return mine + unpack(pass_head_in.at[u, which], pass_rest_in.at[u, which])

    def finish(u, straight=False):
        product = whole(u, LEFT, straight) * whole(u, RIGHT, straight)
        row_sums[u, : quarter // TOKENS, :] = jnp.sum(
            product.reshape(quarter // TOKENS, TOKENS, LANES), axis=1
        )

    def sent(u):
        for which in (LEFT, RIGHT):
            for kind in (RELAY, DIRECT):
                for copy in first_copies(u, which, kind):
                    copy.wait_send()
            for copy in pass_copies(u, which):
                copy.wait_send()

    def block_sent(k):
        for stream in (NEAR, FAR):
            for which in (LEFT, RIGHT):
                block_copy(stream, k, which, partner_id).wait_send()

    def epilogue(tile):
        sums = row_sums[pl.ds(tile * CHUNKS, CHUNKS)].reshape(CHUNKS * TOKENS, LANES)
        result[tile] = exact_dot(row_pick[...], exact_dot(sums, lane_pick[...]) * keep[...])

    swapped = send(result.at[0], landed.at[0], result_send.at[0], result_recv.at[0], partner_id)
    moved = send(result.at[1], landed.at[1], result_send.at[1], result_recv.at[1], next_id)

    row_sums[...] = jnp.zeros_like(row_sums)
    build_picks(even, lane_pick, keep, row_pick)
    for load in loads:
        load.wait()

    @pl.when(even)
    def _():
        @pl.loop(0, CHUNKS)
        def _(k):
            for which in (LEFT, RIGHT):
                wait_block(NEAR, k, which)
                lanes_first(k, which, own[which], chunk_of(NEAR, k, which))
                hand_on(k, which)

            @pl.when(k >= 1)
            def _():
                relay(k - 1, LEFT)
                relay(k - 1, RIGHT)

            @pl.when(k >= 2)
            def _():
                finish(k - 2)

        relay(CHUNKS - 1, LEFT)
        relay(CHUNKS - 1, RIGHT)

        @pl.loop(0, CHUNKS - 1)
        def _(k):
            u = CHUNKS + k
            for which in (LEFT, RIGHT):
                wait_block(FAR, k, which)
                lanes_first(u, which, own[which], chunk_of(FAR, k, which))
                hand_on(u, which)

            @pl.when(k == 1)
            def _():
                finish(CHUNKS - 2)
                finish(CHUNKS - 1)
                epilogue(0)
                swapped.start()

            for which in (LEFT, RIGHT):
                relay(u, which)

            @pl.when(k >= 1)
            def _():
                finish(u - 1)
                sent(k - 1)
                sent(u - 1)
                block_sent(k - 1)

        for which in (LEFT, RIGHT):
            wait_block(FAR, CHUNKS - 1, which)
            chunk = chunk_of(FAR, CHUNKS - 1, which)
            lanes_first(units - 1, which, own[which], chunk)
            hand_on(units - 1, which, straight=True)
        finish(units - 2)
        sent(CHUNKS - 2)
        sent(units - 2)
        block_sent(CHUNKS - 2)
        sent(CHUNKS - 1)
        finish(units - 1, straight=True)
        epilogue(1)
        moved.start()

    @pl.when(odd)
    def _():
        @pl.loop(0, CHUNKS)
        def _(k):
            for which in (LEFT, RIGHT):
                wait_block(NEAR, k, which)

        @pl.loop(0, CHUNKS)
        def _(k):
            for which in (LEFT, RIGHT):
                wait_block(FAR, k, which)
                chunk = chunk_of(FAR, k, which)
                other = got[which].at[NEAR].reshape(block_rows, got[which].shape[-1])
                rows_first(k, which, other, chunk)
                hand_on(k, which)
                rows_first(CHUNKS + k, which, own[which], chunk)
                hand_on(CHUNKS + k, which)

            for which in (LEFT, RIGHT):
                relay(k, which)
                relay(CHUNKS + k, which)

            @pl.when(k >= 1)
            def _():
                finish(k - 1)
                finish(CHUNKS + k - 1)
                sent(k - 1)
                sent(CHUNKS + k - 1)
                block_sent(k - 1)

        finish(CHUNKS - 1)
        epilogue(0)
        swapped.start()
        finish(units - 1)
        epilogue(1)

    block_sent(CHUNKS - 1)
    sent(units - 1)

    @pl.when(odd)
    def _():
        sent(CHUNKS - 1)

    def put(offset, value):
        for i in range(quarter // TOKENS):
            out_ref[i, offset : offset + 1, :] = value[i : i + 1, :]

    @pl.when(odd)
    def _():
        put(1, result[1])

    swapped.wait()
    put(0, landed[0])

    @pl.when(even)
    def _():
        moved.wait()
        put(1, landed[1])


def build_picks(even, lane_pick, keep, row_pick):
    def iota(shape, axis):
        return lax.broadcasted_iota(jnp.int32, shape, axis)

    def twelfth(j):
        return (
            (j >= 12).astype(jnp.int32)
            + (j >= 24).astype(jnp.int32)
            + (j >= 36).astype(jnp.int32)
        )

    held = CHUNKS * TOKENS
    lane, target = iota((LANES, LANES), 0), iota((LANES, LANES), 1)
    group = lane >> 4
    by_rows = jnp.logical_and(group == (target & 7), target < 48).astype(jnp.float32)
    by_lanes = jnp.logical_and(
        group == 2 * twelfth(target) + (target & 1), target < 48
    ).astype(jnp.float32)
    lane_pick[...] = jnp.where(even, by_lanes, by_rows)
    line, target = iota((held, LANES), 0), iota((held, LANES), 1)
    by_rows = (((line & 15) >> 1) == (target >> 3)).astype(jnp.float32)
    by_lanes = (
        (line >> 4) == ((target - 12 * twelfth(target)) >> 1)
    ).astype(jnp.float32)
    keep[...] = jnp.where(even, by_lanes, by_rows)
    out, line = iota((16, held), 0), iota((16, held), 1)
    place = line & 15
    by_rows = jnp.logical_and(
        2 * (line >> 4) + (place & 1) == out, place < 12
    ).astype(jnp.float32)
    by_lanes = jnp.logical_and(place == out, place < 12).astype(jnp.float32)
    row_pick[...] = jnp.where(even, by_lanes, by_rows)


def solution(mesh):
    grid_rows, grid_cols = mesh.shape["row"], mesh.shape["col"]
    placed = (
        P(("row", "col"), None, "tensor"),
        P(("row", "col"), None, "tensor"),
        P(("row", "col"), None),
    )

    def per_device(hidden, cotangent, tile_live):
        samples, tokens, width = hidden.shape
        cotan_width = cotangent.shape[2]
        block_rows = samples * tokens
        quarter = block_rows // PARTS
        piece = quarter // CHUNKS
        units = 2 * CHUNKS
        f32, bf16, i16 = jnp.float32, jnp.bfloat16, jnp.int16
        vmem, dma = pltpu.VMEM, pltpu.SemaphoreType.DMA
        held = pltpu.MemorySpace.HBM
        sums = pl.pallas_call(
            functools.partial(tile_kernel, grid_rows, grid_cols),
            out_shape=jax.ShapeDtypeStruct((samples // PARTS, 2, LANES), f32),
            in_specs=[pl.BlockSpec(memory_space=held)] * 2,
            out_specs=pl.BlockSpec(memory_space=pltpu.VMEM),
            scratch_shapes=[
                vmem((block_rows, width), bf16),
                vmem((block_rows, cotan_width), bf16),
                vmem((2, PARTS, CHUNKS, piece, width), bf16),
                vmem((2, PARTS, CHUNKS, piece, cotan_width), bf16),
                vmem((units, 2, PARTS, quarter, LANES), f32),
                vmem((units, 2, 2, quarter, LANES), bf16),
                vmem((units, 2, 2, quarter // 2, LANES), i16),
                vmem((units, 2, 2, quarter, LANES), bf16),
                vmem((units, 2, 2, quarter // 2, LANES), i16),
                vmem((units, 2, quarter, LANES), bf16),
                vmem((units, 2, quarter // 2, LANES), i16),
                vmem((units, 2, quarter, LANES), bf16),
                vmem((units, 2, quarter // 2, LANES), i16),
                vmem((units, TOKENS, LANES), f32),
                vmem((LANES, LANES), f32),
                vmem((CHUNKS * TOKENS, LANES), f32),
                vmem((TOKENS, CHUNKS * TOKENS), f32),
                vmem((2, TOKENS, LANES), f32),
                vmem((2, TOKENS, LANES), f32),
                dma((2,)),
                dma((2, CHUNKS, 2)),
                dma((2, CHUNKS, 2)),
                dma((units, 2, 2, 2)),
                dma((units, 2, 2, 2)),
                dma((units, 2, 2)),
                dma((units, 2, 2)),
                dma((2,)),
                dma((2,)),
            ],
            compiler_params=pltpu.CompilerParams(
                collective_id=0,
                has_side_effects=True,
                vmem_limit_bytes=60 * 1024 * 1024,
            ),
        )(
            hidden.reshape(PARTS, CHUNKS, piece, width),
            cotangent.reshape(PARTS, CHUNKS, piece, cotan_width),
        )
        kernel_scale = 1.0 / (tokens * math.sqrt(FF * D))
        values = sums[:, :, :samples] * kernel_scale
        live = lax.broadcast_in_dim(tile_live[0], values.shape, (1,))
        return jnp.transpose(values * live.astype(f32), (1, 0, 2))[None]

    return jax.shard_map(
        per_device,
        mesh=mesh,
        in_specs=placed,
        out_specs=P(("row", "col"), None, "tensor", None),
        check_vma=False,
    )
```

```python
import functools
import math

import jax
import jax.numpy as jnp
from jax import lax
from jax.experimental import pallas as pl
from jax.experimental.pallas import tpu as pltpu
from jax.sharding import PartitionSpec as P

D = 4096
FF = 11008
CHUNKS = 6
PARTS = 4
LANES = 128
TOKENS = 16
NEAR, FAR = 0, 1
RELAY, DIRECT = 0, 1
STEPS = 127.0 * 256.0
LEFT, RIGHT = 0, 1


def contract(rows, columns):
    return lax.dot_general(
        rows, columns, (((1,), (1,)), ((), ())), preferred_element_type=jnp.float32
    )


def exact_dot(a, b):
    return jnp.dot(
        a, b, precision=lax.Precision.HIGHEST, preferred_element_type=jnp.float32
    )


def pack(value, head_ref, rest_ref):
    half = value.shape[0] // 2
    head = value.astype(jnp.bfloat16)
    wide = head.astype(jnp.float32)
    rest = jnp.round((value - wide) * (STEPS / jnp.maximum(jnp.abs(wide), 1e-30)))
    both = rest[:half] * 256.0 + rest[half:]
    head_ref[...] = head
    rest_ref[...] = both.astype(jnp.int32).astype(jnp.int16)


def unpack(head_ref, rest_ref):
    wide = head_ref[...].astype(jnp.float32)
    both = rest_ref[...].astype(jnp.int32).astype(jnp.float32)
    first = jnp.floor((both + 128.0) * (1.0 / 256.0))
    rest = jnp.concatenate([first, both - 256.0 * first], axis=0)
    return wide + jnp.abs(wide) * (rest * (1.0 / STEPS))


def tile_kernel(
    grid_rows,
    grid_cols,
    kernel_scale,
    live_ref,
    hidden_ref,
    cotan_ref,
    out_ref,
    own_hidden,
    own_cotan,
    got_hidden,
    got_cotan,
    edge,
    edge_in,
    gram,
    first_head,
    first_rest,
    first_head_in,
    first_rest_in,
    pass_head,
    pass_rest,
    pass_head_in,
    pass_rest_in,
    row_sums,
    lane_pick,
    keep,
    row_pick,
    result,
    landed,
    load_sem,
    edge_send,
    edge_recv,
    block_send,
    got_sem,
    first_send,
    first_recv,
    pass_send,
    pass_recv,
    result_send,
    result_recv,
):
    row = lax.axis_index("row")
    col = lax.axis_index("col")
    me = lax.axis_index("tensor")
    core = lax.rem(col, 2)
    even = core == 0
    odd = core == 1
    units = 2 * CHUNKS
    block_rows = own_hidden.shape[0]
    quarter = block_rows // PARTS
    piece = quarter // CHUNKS
    half_rows = block_rows // 2
    even_width = hidden_ref.shape[-1] // LANES * LANES
    spare = hidden_ref.shape[-1] - even_width
    assert 2 * spare == LANES

    up = lax.rem(me + 1, PARTS)
    down = lax.rem(me + PARTS - 1, PARTS)
    across = lax.rem(me + 2, PARTS)
    up_id = (row, col, up)
    down_id = (row, col, down)
    across_id = (row, col, across)
    partner_id = (row, col + 1 - 2 * core, me)
    next_id = (
        lax.rem(row + (col + 2) // grid_cols, grid_rows),
        lax.rem(col + 2, grid_cols),
        me,
    )
    prev_id = (
        lax.rem(row + grid_rows - 1 + (col + grid_cols - 2) // grid_cols, grid_rows),
        lax.rem(col + grid_cols - 2, grid_cols),
        me,
    )
    far_id = tuple(jnp.where(even, p, n) for p, n in zip(prev_id, next_id))

    def by_piece(own):
        return own.reshape(PARTS, CHUNKS, piece, own.shape[-1])

    loads = (
        pltpu.make_async_copy(hidden_ref, by_piece(own_hidden), load_sem.at[0]),
        pltpu.make_async_copy(cotan_ref, by_piece(own_cotan), load_sem.at[1]),
    )
    for load in loads:
        load.start()

    barrier = pltpu.get_barrier_semaphore()
    peers = (up_id, down_id, across_id, partner_id, next_id, prev_id)
    for peer in peers:
        pl.semaphore_signal(
            barrier, inc=1, device_id=peer, device_id_type=pl.DeviceIdType.MESH
        )
    pl.semaphore_wait(barrier, len(peers))

    def send(source, target, send_sem, recv_sem, device):
        return pltpu.make_async_remote_copy(
            src_ref=source,
            dst_ref=target,
            send_sem=send_sem,
            recv_sem=recv_sem,
            device_id=device,
            device_id_type=pl.DeviceIdType.MESH,
        )

    def block_copy(stream, k, which, device):
        source, target = ((hidden_ref, got_hidden), (cotan_ref, got_cotan))[which]
        source, target = source.at[:, k], target.at[stream, :, k]
        if stream == FAR and which == LEFT:
            source, target = source.at[:, :, :even_width], target.at[:, :, :even_width]
        return send(
            source,
            target,
            block_send.at[stream, k, which],
            got_sem.at[stream, k, which],
            device,
        )

    edge_copy = send(edge, edge_in, edge_send, edge_recv, far_id)

    for which in (LEFT, RIGHT):
        block_copy(FAR, 0, which, far_id).start()

    @pl.loop(0, CHUNKS)
    def _(k):
        for which in (LEFT, RIGHT):
            block_copy(NEAR, k, which, partner_id).start()

    for load in loads:
        load.wait()
    edge[...] = jnp.concatenate(
        [own_hidden[:half_rows, even_width:], own_hidden[half_rows:, even_width:]],
        axis=1,
    )
    edge_copy.start()

    @pl.loop(1, CHUNKS)
    def _(k):
        for which in (LEFT, RIGHT):
            block_copy(FAR, k, which, far_id).start()

    def place_edge():
        edge_copy.wait()
        for half in range(2):
            columns = edge_in[:, half * spare : (half + 1) * spare]
            got_hidden[FAR, 2 * half : 2 * half + 2, :, :, even_width:] = columns.reshape(
                2, CHUNKS, piece, spare
            )

    def wait_block(stream, k, which):
        block_copy(stream, k, which, partner_id).wait_recv()

    ways = ((up, up_id, down, down_id), (down, down_id, up, up_id))

    def first_copies(u, which, kind):
        device = ways[which][1 + 2 * kind]
        return (
            send(first_head.at[u, which, kind], first_head_in.at[u, which, kind], first_send.at[u, which, kind, 0], first_recv.at[u, which, kind, 0], device),
            send(first_rest.at[u, which, kind], first_rest_in.at[u, which, kind], first_send.at[u, which, kind, 1], first_recv.at[u, which, kind, 1], device),
        )

    def pass_copies(u, which, straight=False):
        device = across_id if straight else ways[which][1]
        return (
            send(pass_head.at[u, which], pass_head_in.at[u, which], pass_send.at[u, which, 0], pass_recv.at[u, which, 0], device),
            send(pass_rest.at[u, which], pass_rest_in.at[u, which], pass_send.at[u, which, 1], pass_recv.at[u, which, 1], device),
        )

    own = (own_hidden, own_cotan)
    got = (got_hidden, got_cotan)

    def chunk_of(stream, k, which):
        return got[which][stream, :, k].reshape(PARTS * piece, got[which].shape[-1])

    def lanes_first(u, which, rows, chunk):
        for part in range(PARTS):
            gram[u, which, part] = contract(
                rows[part * quarter : (part + 1) * quarter, :], chunk
            )

    def rows_first(u, which, columns, chunk):
        wide = 2 * LANES
        for block in range(block_rows // wide):
            value = contract(chunk, columns[block * wide : (block + 1) * wide, :])
            for part in range(PARTS):
                for half in range(2):
                    start = (2 * block + half) * piece
                    gram[u, which, part, start : start + piece, :] = value[
                        part * piece : (part + 1) * piece,
                        half * LANES : (half + 1) * LANES,
                    ]

    def hand_on(u, which, straight=False):
        if straight:
            pack(gram[u, which, across], pass_head.at[u, which], pass_rest.at[u, which])
            for copy in pass_copies(u, which, straight):
                copy.start()
        relayed = ways[which][0] if straight else across
        for kind, part in ((RELAY, relayed), (DIRECT, ways[which][2])):
            pack(
                gram[u, which, part],
                first_head.at[u, which, kind],
                first_rest.at[u, which, kind],
            )
            for copy in first_copies(u, which, kind):
                copy.start()

    def relay(u, which):
        for copy in first_copies(u, which, RELAY):
            copy.wait_recv()
        total = gram[u, which, ways[which][0]] + unpack(
            first_head_in.at[u, which, RELAY], first_rest_in.at[u, which, RELAY]
        )
        pack(total, pass_head.at[u, which], pass_rest.at[u, which])
        for copy in pass_copies(u, which):
            copy.start()

    def whole(u, which, straight=False):
        for copy in first_copies(u, which, DIRECT):
            copy.wait_recv()
        direct = unpack(
            first_head_in.at[u, which, DIRECT], first_rest_in.at[u, which, DIRECT]
        )
        mine = gram[u, which, me] + direct
        if straight:
            for copy in first_copies(u, which, RELAY):
                copy.wait_recv()
            mine = mine + unpack(
                first_head_in.at[u, which, RELAY], first_rest_in.at[u, which, RELAY]
            )
        for copy in pass_copies(u, which):
            copy.wait_recv()
        return mine + unpack(pass_head_in.at[u, which], pass_rest_in.at[u, which])

    def finish(u, straight=False):
        product = whole(u, LEFT, straight) * whole(u, RIGHT, straight)
        row_sums[u, : quarter // TOKENS, :] = jnp.sum(
            product.reshape(quarter // TOKENS, TOKENS, LANES), axis=1
        )

    def sent(u):
        for which in (LEFT, RIGHT):
            for kind in (RELAY, DIRECT):
                for copy in first_copies(u, which, kind):
                    copy.wait_send()
            for copy in pass_copies(u, which):
                copy.wait_send()

    def block_sent(k):
        for stream in (NEAR, FAR):
            for which in (LEFT, RIGHT):
                block_copy(stream, k, which, partner_id).wait_send()

    def epilogue(tile):
        sums = row_sums[pl.ds(tile * CHUNKS, CHUNKS)].reshape(CHUNKS * TOKENS, LANES)
        result[tile] = exact_dot(row_pick[...], exact_dot(sums, lane_pick[...]) * keep[...])

    swapped = send(result.at[0], landed.at[0], result_send.at[0], result_recv.at[0], partner_id)
    moved = send(result.at[1], landed.at[1], result_send.at[1], result_recv.at[1], next_id)

    row_sums[...] = jnp.zeros_like(row_sums)
    build_picks(even, lane_pick, keep, row_pick)

    @pl.when(even)
    def _():
        @pl.loop(0, CHUNKS)
        def _(k):
            for which in (LEFT, RIGHT):
                wait_block(NEAR, k, which)
                lanes_first(k, which, own[which], chunk_of(NEAR, k, which))
                hand_on(k, which)

            @pl.when(k >= 1)
            def _():
                relay(k - 1, LEFT)
                relay(k - 1, RIGHT)

            @pl.when(k >= 2)
            def _():
                finish(k - 2)

        relay(CHUNKS - 1, LEFT)
        relay(CHUNKS - 1, RIGHT)

        place_edge()

        @pl.loop(0, CHUNKS - 1)
        def _(k):
            u = CHUNKS + k
            for which in (LEFT, RIGHT):
                wait_block(FAR, k, which)
                lanes_first(u, which, own[which], chunk_of(FAR, k, which))
                hand_on(u, which)

            @pl.when(k == 1)
            def _():
                finish(CHUNKS - 2)
                finish(CHUNKS - 1)
                epilogue(0)
                swapped.start()

            for which in (LEFT, RIGHT):
                relay(u, which)

            @pl.when(k >= 1)
            def _():
                finish(u - 1)
                sent(k - 1)
                sent(u - 1)
                block_sent(k - 1)

        for which in (LEFT, RIGHT):
            wait_block(FAR, CHUNKS - 1, which)
            chunk = chunk_of(FAR, CHUNKS - 1, which)
            lanes_first(units - 1, which, own[which], chunk)
            hand_on(units - 1, which, straight=True)
        finish(units - 2)
        sent(CHUNKS - 2)
        sent(units - 2)
        block_sent(CHUNKS - 2)
        sent(CHUNKS - 1)
        finish(units - 1, straight=True)
        epilogue(1)
        moved.start()

    @pl.when(odd)
    def _():
        @pl.loop(0, CHUNKS)
        def _(k):
            for which in (LEFT, RIGHT):
                wait_block(NEAR, k, which)

        place_edge()

        @pl.loop(0, CHUNKS)
        def _(k):
            for which in (LEFT, RIGHT):
                wait_block(FAR, k, which)
                chunk = chunk_of(FAR, k, which)
                other = got[which].at[NEAR].reshape(block_rows, got[which].shape[-1])
                rows_first(k, which, other, chunk)
                hand_on(k, which)
                rows_first(CHUNKS + k, which, own[which], chunk)
                hand_on(CHUNKS + k, which)

            for which in (LEFT, RIGHT):
                relay(k, which)
                relay(CHUNKS + k, which)

            @pl.when(k >= 1)
            def _():
                finish(k - 1)
                finish(CHUNKS + k - 1)
                sent(k - 1)
                sent(CHUNKS + k - 1)
                block_sent(k - 1)

        finish(CHUNKS - 1)
        epilogue(0)
        swapped.start()
        finish(units - 1)
        epilogue(1)

    block_sent(CHUNKS - 1)
    sent(units - 1)

    @pl.when(odd)
    def _():
        sent(CHUNKS - 1)

    def put(offset, value):
        value = value * (live_ref[0, offset].astype(jnp.float32) * kernel_scale)
        for i in range(quarter // TOKENS):
            out_ref[i, offset : offset + 1, :] = value[i : i + 1, :]

    @pl.when(odd)
    def _():
        put(1, result[1])

    swapped.wait()
    put(0, landed[0])

    @pl.when(even)
    def _():
        moved.wait()
        put(1, landed[1])


def build_picks(even, lane_pick, keep, row_pick):
    def iota(shape, axis):
        return lax.broadcasted_iota(jnp.int32, shape, axis)

    def twelfth(j):
        return (
            (j >= 12).astype(jnp.int32)
            + (j >= 24).astype(jnp.int32)
            + (j >= 36).astype(jnp.int32)
        )

    held = CHUNKS * TOKENS
    lane, target = iota((LANES, LANES), 0), iota((LANES, LANES), 1)
    group = lane >> 4
    by_rows = jnp.logical_and(group == (target & 7), target < 48).astype(jnp.float32)
    by_lanes = jnp.logical_and(
        group == 2 * twelfth(target) + (target & 1), target < 48
    ).astype(jnp.float32)
    lane_pick[...] = jnp.where(even, by_lanes, by_rows)
    line, target = iota((held, LANES), 0), iota((held, LANES), 1)
    by_rows = (((line & 15) >> 1) == (target >> 3)).astype(jnp.float32)
    by_lanes = (
        (line >> 4) == ((target - 12 * twelfth(target)) >> 1)
    ).astype(jnp.float32)
    keep[...] = jnp.where(even, by_lanes, by_rows)
    out, line = iota((16, held), 0), iota((16, held), 1)
    place = line & 15
    by_rows = jnp.logical_and(
        2 * (line >> 4) + (place & 1) == out, place < 12
    ).astype(jnp.float32)
    by_lanes = jnp.logical_and(place == out, place < 12).astype(jnp.float32)
    row_pick[...] = jnp.where(even, by_lanes, by_rows)


def solution(mesh):
    grid_rows, grid_cols = mesh.shape["row"], mesh.shape["col"]
    placed = (
        P(("row", "col"), None, "tensor"),
        P(("row", "col"), None, "tensor"),
        P(("row", "col"), None),
    )

    def per_device(hidden, cotangent, tile_live):
        samples, tokens, width = hidden.shape
        cotan_width = cotangent.shape[2]
        block_rows = samples * tokens
        quarter = block_rows // PARTS
        piece = quarter // CHUNKS
        units = 2 * CHUNKS
        f32, bf16, i16 = jnp.float32, jnp.bfloat16, jnp.int16
        vmem, dma = pltpu.VMEM, pltpu.SemaphoreType.DMA
        held = pltpu.MemorySpace.HBM
        kernel_scale = 1.0 / (tokens * math.sqrt(FF * D))
        sums = pl.pallas_call(
            functools.partial(tile_kernel, grid_rows, grid_cols, kernel_scale),
            out_shape=jax.ShapeDtypeStruct((samples // PARTS, 2, LANES), f32),
            in_specs=[pl.BlockSpec(memory_space=pltpu.SMEM)]
            + [pl.BlockSpec(memory_space=held)] * 2,
            out_specs=pl.BlockSpec(memory_space=pltpu.VMEM),
            scratch_shapes=[
                vmem((block_rows, width), bf16),
                vmem((block_rows, cotan_width), bf16),
                vmem((2, PARTS, CHUNKS, piece, width), bf16),
                vmem((2, PARTS, CHUNKS, piece, cotan_width), bf16),
                vmem((block_rows // 2, LANES), bf16),
                vmem((block_rows // 2, LANES), bf16),
                vmem((units, 2, PARTS, quarter, LANES), f32),
                vmem((units, 2, 2, quarter, LANES), bf16),
                vmem((units, 2, 2, quarter // 2, LANES), i16),
                vmem((units, 2, 2, quarter, LANES), bf16),
                vmem((units, 2, 2, quarter // 2, LANES), i16),
                vmem((units, 2, quarter, LANES), bf16),
                vmem((units, 2, quarter // 2, LANES), i16),
                vmem((units, 2, quarter, LANES), bf16),
                vmem((units, 2, quarter // 2, LANES), i16),
                vmem((units, TOKENS, LANES), f32),
                vmem((LANES, LANES), f32),
                vmem((CHUNKS * TOKENS, LANES), f32),
                vmem((TOKENS, CHUNKS * TOKENS), f32),
                vmem((2, TOKENS, LANES), f32),
                vmem((2, TOKENS, LANES), f32),
                dma((2,)),
                dma,
                dma,
                dma((2, CHUNKS, 2)),
                dma((2, CHUNKS, 2)),
                dma((units, 2, 2, 2)),
                dma((units, 2, 2, 2)),
                dma((units, 2, 2)),
                dma((units, 2, 2)),
                dma((2,)),
                dma((2,)),
            ],
            compiler_params=pltpu.CompilerParams(
                collective_id=0,
                has_side_effects=True,
                vmem_limit_bytes=60 * 1024 * 1024,
            ),
        )(
            tile_live,
            hidden.reshape(PARTS, CHUNKS, piece, width),
            cotangent.reshape(PARTS, CHUNKS, piece, cotan_width),
        )
        return jnp.transpose(sums[:, :, :samples], (1, 0, 2))[None]

    return jax.shard_map(
        per_device,
        mesh=mesh,
        in_specs=placed,
        out_specs=P(("row", "col"), None, "tensor", None),
        check_vma=False,
    )
```

```python
import functools
import math

import jax
import jax.numpy as jnp
from jax import lax
from jax.experimental import pallas as pl
from jax.experimental.pallas import tpu as pltpu
from jax.sharding import PartitionSpec as P

D = 4096
FF = 11008
CHUNKS = 6
PARTS = 4
LANES = 128
TOKENS = 16
NEAR, FAR = 0, 1
RELAY, DIRECT = 0, 1
STEPS = 127.0 * 256.0
LEFT, RIGHT = 0, 1


def contract(rows, columns):
    return lax.dot_general(
        rows, columns, (((1,), (1,)), ((), ())), preferred_element_type=jnp.float32
    )


def exact_dot(a, b):
    return jnp.dot(
        a, b, precision=lax.Precision.HIGHEST, preferred_element_type=jnp.float32
    )


def pack(value, head_ref, rest_ref):
    half = value.shape[0] // 2
    head = value.astype(jnp.bfloat16)
    wide = head.astype(jnp.float32)
    rest = jnp.round((value - wide) * (STEPS / jnp.maximum(jnp.abs(wide), 1e-30)))
    both = rest[:half] * 256.0 + rest[half:]
    head_ref[...] = head
    rest_ref[...] = both.astype(jnp.int32).astype(jnp.int16)


def unpack(head_ref, rest_ref):
    wide = head_ref[...].astype(jnp.float32)
    both = rest_ref[...].astype(jnp.int32).astype(jnp.float32)
    first = jnp.floor((both + 128.0) * (1.0 / 256.0))
    rest = jnp.concatenate([first, both - 256.0 * first], axis=0)
    return wide + jnp.abs(wide) * (rest * (1.0 / STEPS))


def tile_kernel(
    grid_rows,
    grid_cols,
    kernel_scale,
    live_ref,
    hidden_ref,
    cotan_ref,
    out_ref,
    own_hidden,
    own_cotan,
    got_hidden,
    got_cotan,
    edge,
    edge_in,
    gram,
    first_head,
    first_rest,
    first_head_in,
    first_rest_in,
    pass_head,
    pass_rest,
    pass_head_in,
    pass_rest_in,
    row_sums,
    lane_pick,
    keep,
    row_pick,
    result,
    landed,
    load_sem,
    edge_send,
    edge_recv,
    block_send,
    got_sem,
    first_send,
    first_recv,
    pass_send,
    pass_recv,
    result_send,
    result_recv,
):
    row = lax.axis_index("row")
    col = lax.axis_index("col")
    me = lax.axis_index("tensor")
    core = lax.rem(col, 2)
    even = core == 0
    odd = core == 1
    units = 2 * CHUNKS
    block_rows = own_hidden.shape[0]
    quarter = block_rows // PARTS
    piece = quarter // CHUNKS
    half_rows = block_rows // 2
    even_width = hidden_ref.shape[-1] // LANES * LANES
    spare = hidden_ref.shape[-1] - even_width
    assert 2 * spare == LANES

    up = lax.rem(me + 1, PARTS)
    down = lax.rem(me + PARTS - 1, PARTS)
    across = lax.rem(me + 2, PARTS)
    up_id = (row, col, up)
    down_id = (row, col, down)
    across_id = (row, col, across)
    partner_id = (row, col + 1 - 2 * core, me)
    next_id = (
        lax.rem(row + (col + 2) // grid_cols, grid_rows),
        lax.rem(col + 2, grid_cols),
        me,
    )
    prev_id = (
        lax.rem(row + grid_rows - 1 + (col + grid_cols - 2) // grid_cols, grid_rows),
        lax.rem(col + grid_cols - 2, grid_cols),
        me,
    )
    far_id = tuple(jnp.where(even, p, n) for p, n in zip(prev_id, next_id))

    def by_piece(own):
        return own.reshape(PARTS, CHUNKS, piece, own.shape[-1])

    loads = (
        pltpu.make_async_copy(hidden_ref, by_piece(own_hidden), load_sem.at[0]),
        pltpu.make_async_copy(cotan_ref, by_piece(own_cotan), load_sem.at[1]),
    )
    for load in loads:
        load.start()

    barrier = pltpu.get_barrier_semaphore()
    peers = (up_id, down_id, across_id, partner_id, next_id, prev_id)
    for peer in peers:
        pl.semaphore_signal(
            barrier, inc=1, device_id=peer, device_id_type=pl.DeviceIdType.MESH
        )
    pl.semaphore_wait(barrier, len(peers))

    def send(source, target, send_sem, recv_sem, device):
        return pltpu.make_async_remote_copy(
            src_ref=source,
            dst_ref=target,
            send_sem=send_sem,
            recv_sem=recv_sem,
            device_id=device,
            device_id_type=pl.DeviceIdType.MESH,
        )

    def block_copy(stream, k, which, device):
        source, target = ((hidden_ref, got_hidden), (cotan_ref, got_cotan))[which]
        source, target = source.at[:, k], target.at[stream, :, k]
        if stream == FAR and which == LEFT:
            source, target = source.at[:, :, :even_width], target.at[:, :, :even_width]
        return send(
            source,
            target,
            block_send.at[stream, k, which],
            got_sem.at[stream, k, which],
            device,
        )

    edge_copy = send(edge, edge_in, edge_send, edge_recv, far_id)

    for which in (RIGHT, LEFT):
        block_copy(FAR, 0, which, far_id).start()

    @pl.loop(0, CHUNKS)
    def _(k):
        for which in (RIGHT, LEFT):
            block_copy(NEAR, k, which, partner_id).start()

    for load in loads:
        load.wait()
    edge[...] = jnp.concatenate(
        [own_hidden[:half_rows, even_width:], own_hidden[half_rows:, even_width:]],
        axis=1,
    )
    edge_copy.start()

    @pl.loop(1, CHUNKS)
    def _(k):
        for which in (RIGHT, LEFT):
            block_copy(FAR, k, which, far_id).start()

    def place_edge():
        edge_copy.wait()
        for half in range(2):
            columns = edge_in[:, half * spare : (half + 1) * spare]
            got_hidden[FAR, 2 * half : 2 * half + 2, :, :, even_width:] = columns.reshape(
                2, CHUNKS, piece, spare
            )

    def wait_block(stream, k, which):
        block_copy(stream, k, which, partner_id).wait_recv()

    ways = ((up, up_id, down, down_id), (down, down_id, up, up_id))

    def first_copies(u, which, kind):
        device = ways[which][1 + 2 * kind]
        return (
            send(first_head.at[u, which, kind], first_head_in.at[u, which, kind], first_send.at[u, which, kind, 0], first_recv.at[u, which, kind, 0], device),
            send(first_rest.at[u, which, kind], first_rest_in.at[u, which, kind], first_send.at[u, which, kind, 1], first_recv.at[u, which, kind, 1], device),
        )

    def pass_copies(u, which, straight=False):
        device = across_id if straight else ways[which][1]
        return (
            send(pass_head.at[u, which], pass_head_in.at[u, which], pass_send.at[u, which, 0], pass_recv.at[u, which, 0], device),
            send(pass_rest.at[u, which], pass_rest_in.at[u, which], pass_send.at[u, which, 1], pass_recv.at[u, which, 1], device),
        )

    own = (own_hidden, own_cotan)
    got = (got_hidden, got_cotan)

    def chunk_of(stream, k, which):
        return got[which][stream, :, k].reshape(PARTS * piece, got[which].shape[-1])

    def lanes_first(u, which, rows, chunk):
        for part in range(PARTS):
            gram[u, which, part] = contract(
                rows[part * quarter : (part + 1) * quarter, :], chunk
            )

    def rows_first(u, which, columns, chunk):
        wide = 2 * LANES
        for block in range(block_rows // wide):
            value = contract(chunk, columns[block * wide : (block + 1) * wide, :])
            for part in range(PARTS):
                for half in range(2):
                    start = (2 * block + half) * piece
                    gram[u, which, part, start : start + piece, :] = value[
                        part * piece : (part + 1) * piece,
                        half * LANES : (half + 1) * LANES,
                    ]

    def hand_on(u, which, straight=False):
        if straight:
            pack(gram[u, which, across], pass_head.at[u, which], pass_rest.at[u, which])
            for copy in pass_copies(u, which, straight):
                copy.start()
        relayed = ways[which][0] if straight else across
        for kind, part in ((RELAY, relayed), (DIRECT, ways[which][2])):
            pack(
                gram[u, which, part],
                first_head.at[u, which, kind],
                first_rest.at[u, which, kind],
            )
            for copy in first_copies(u, which, kind):
                copy.start()

    def relay(u, which):
        for copy in first_copies(u, which, RELAY):
            copy.wait_recv()
        total = gram[u, which, ways[which][0]] + unpack(
            first_head_in.at[u, which, RELAY], first_rest_in.at[u, which, RELAY]
        )
        pack(total, pass_head.at[u, which], pass_rest.at[u, which])
        for copy in pass_copies(u, which):
            copy.start()

    def whole(u, which, straight=False):
        for copy in first_copies(u, which, DIRECT):
            copy.wait_recv()
        direct = unpack(
            first_head_in.at[u, which, DIRECT], first_rest_in.at[u, which, DIRECT]
        )
        mine = gram[u, which, me] + direct
        if straight:
            for copy in first_copies(u, which, RELAY):
                copy.wait_recv()
            mine = mine + unpack(
                first_head_in.at[u, which, RELAY], first_rest_in.at[u, which, RELAY]
            )
        for copy in pass_copies(u, which):
            copy.wait_recv()
        return mine + unpack(pass_head_in.at[u, which], pass_rest_in.at[u, which])

    def finish(u, straight=False):
        product = whole(u, LEFT, straight) * whole(u, RIGHT, straight)
        row_sums[u, : quarter // TOKENS, :] = jnp.sum(
            product.reshape(quarter // TOKENS, TOKENS, LANES), axis=1
        )

    def sent(u):
        for which in (RIGHT, LEFT):
            for kind in (RELAY, DIRECT):
                for copy in first_copies(u, which, kind):
                    copy.wait_send()
            for copy in pass_copies(u, which):
                copy.wait_send()

    def block_sent(k):
        for stream in (NEAR, FAR):
            for which in (RIGHT, LEFT):
                block_copy(stream, k, which, partner_id).wait_send()

    def epilogue(tile):
        sums = row_sums[pl.ds(tile * CHUNKS, CHUNKS)].reshape(CHUNKS * TOKENS, LANES)
        result[tile] = exact_dot(row_pick[...], exact_dot(sums, lane_pick[...]) * keep[...])

    swapped = send(result.at[0], landed.at[0], result_send.at[0], result_recv.at[0], partner_id)
    moved = send(result.at[1], landed.at[1], result_send.at[1], result_recv.at[1], next_id)

    row_sums[...] = jnp.zeros_like(row_sums)
    build_picks(even, lane_pick, keep, row_pick)

    @pl.when(even)
    def _():
        @pl.loop(0, CHUNKS)
        def _(k):
            for which in (RIGHT, LEFT):
                wait_block(NEAR, k, which)
                lanes_first(k, which, own[which], chunk_of(NEAR, k, which))
                hand_on(k, which)

            @pl.when(k >= 1)
            def _():
                relay(k - 1, LEFT)
                relay(k - 1, RIGHT)

            @pl.when(k >= 2)
            def _():
                finish(k - 2)

        relay(CHUNKS - 1, LEFT)
        relay(CHUNKS - 1, RIGHT)

        place_edge()

        @pl.loop(0, CHUNKS - 1)
        def _(k):
            u = CHUNKS + k
            for which in (RIGHT, LEFT):
                wait_block(FAR, k, which)
                lanes_first(u, which, own[which], chunk_of(FAR, k, which))
                hand_on(u, which)

            @pl.when(k == 1)
            def _():
                finish(CHUNKS - 2)
                finish(CHUNKS - 1)
                epilogue(0)
                swapped.start()

            for which in (RIGHT, LEFT):
                relay(u, which)

            @pl.when(k >= 1)
            def _():
                finish(u - 1)
                sent(k - 1)
                sent(u - 1)
                block_sent(k - 1)

        for which in (RIGHT, LEFT):
            wait_block(FAR, CHUNKS - 1, which)
            chunk = chunk_of(FAR, CHUNKS - 1, which)
            lanes_first(units - 1, which, own[which], chunk)
            hand_on(units - 1, which, straight=True)
        finish(units - 2)
        sent(CHUNKS - 2)
        sent(units - 2)
        block_sent(CHUNKS - 2)
        sent(CHUNKS - 1)
        finish(units - 1, straight=True)
        epilogue(1)
        moved.start()

    @pl.when(odd)
    def _():
        @pl.loop(0, CHUNKS)
        def _(k):
            for which in (RIGHT, LEFT):
                wait_block(NEAR, k, which)

        place_edge()

        @pl.loop(0, CHUNKS)
        def _(k):
            for which in (RIGHT, LEFT):
                wait_block(FAR, k, which)
                chunk = chunk_of(FAR, k, which)
                other = got[which].at[NEAR].reshape(block_rows, got[which].shape[-1])
                rows_first(k, which, other, chunk)
                hand_on(k, which)
                rows_first(CHUNKS + k, which, own[which], chunk)
                hand_on(CHUNKS + k, which)

            for which in (RIGHT, LEFT):
                relay(k, which)
                relay(CHUNKS + k, which)

            @pl.when(k >= 1)
            def _():
                finish(k - 1)
                finish(CHUNKS + k - 1)
                sent(k - 1)
                sent(CHUNKS + k - 1)
                block_sent(k - 1)

        finish(CHUNKS - 1)
        epilogue(0)
        swapped.start()
        finish(units - 1)
        epilogue(1)

    block_sent(CHUNKS - 1)
    sent(units - 1)

    @pl.when(odd)
    def _():
        sent(CHUNKS - 1)

    def put(offset, value):
        value = value * (live_ref[0, offset].astype(jnp.float32) * kernel_scale)
        for i in range(quarter // TOKENS):
            out_ref[i, offset : offset + 1, :] = value[i : i + 1, :]

    @pl.when(odd)
    def _():
        put(1, result[1])

    swapped.wait()
    put(0, landed[0])

    @pl.when(even)
    def _():
        moved.wait()
        put(1, landed[1])


def build_picks(even, lane_pick, keep, row_pick):
    def iota(shape, axis):
        return lax.broadcasted_iota(jnp.int32, shape, axis)

    def twelfth(j):
        return (
            (j >= 12).astype(jnp.int32)
            + (j >= 24).astype(jnp.int32)
            + (j >= 36).astype(jnp.int32)
        )

    held = CHUNKS * TOKENS
    lane, target = iota((LANES, LANES), 0), iota((LANES, LANES), 1)
    group = lane >> 4
    by_rows = jnp.logical_and(group == (target & 7), target < 48).astype(jnp.float32)
    by_lanes = jnp.logical_and(
        group == 2 * twelfth(target) + (target & 1), target < 48
    ).astype(jnp.float32)
    lane_pick[...] = jnp.where(even, by_lanes, by_rows)
    line, target = iota((held, LANES), 0), iota((held, LANES), 1)
    by_rows = (((line & 15) >> 1) == (target >> 3)).astype(jnp.float32)
    by_lanes = (
        (line >> 4) == ((target - 12 * twelfth(target)) >> 1)
    ).astype(jnp.float32)
    keep[...] = jnp.where(even, by_lanes, by_rows)
    out, line = iota((16, held), 0), iota((16, held), 1)
    place = line & 15
    by_rows = jnp.logical_and(
        2 * (line >> 4) + (place & 1) == out, place < 12
    ).astype(jnp.float32)
    by_lanes = jnp.logical_and(place == out, place < 12).astype(jnp.float32)
    row_pick[...] = jnp.where(even, by_lanes, by_rows)


def solution(mesh):
    grid_rows, grid_cols = mesh.shape["row"], mesh.shape["col"]
    placed = (
        P(("row", "col"), None, "tensor"),
        P(("row", "col"), None, "tensor"),
        P(("row", "col"), None),
    )

    def per_device(hidden, cotangent, tile_live):
        samples, tokens, width = hidden.shape
        cotan_width = cotangent.shape[2]
        block_rows = samples * tokens
        quarter = block_rows // PARTS
        piece = quarter // CHUNKS
        units = 2 * CHUNKS
        f32, bf16, i16 = jnp.float32, jnp.bfloat16, jnp.int16
        vmem, dma = pltpu.VMEM, pltpu.SemaphoreType.DMA
        held = pltpu.MemorySpace.HBM
        kernel_scale = 1.0 / (tokens * math.sqrt(FF * D))
        sums = pl.pallas_call(
            functools.partial(tile_kernel, grid_rows, grid_cols, kernel_scale),
            out_shape=jax.ShapeDtypeStruct((samples // PARTS, 2, LANES), f32),
            in_specs=[pl.BlockSpec(memory_space=pltpu.SMEM)]
            + [pl.BlockSpec(memory_space=held)] * 2,
            out_specs=pl.BlockSpec(memory_space=pltpu.VMEM),
            scratch_shapes=[
                vmem((block_rows, width), bf16),
                vmem((block_rows, cotan_width), bf16),
                vmem((2, PARTS, CHUNKS, piece, width), bf16),
                vmem((2, PARTS, CHUNKS, piece, cotan_width), bf16),
                vmem((block_rows // 2, LANES), bf16),
                vmem((block_rows // 2, LANES), bf16),
                vmem((units, 2, PARTS, quarter, LANES), f32),
                vmem((units, 2, 2, quarter, LANES), bf16),
                vmem((units, 2, 2, quarter // 2, LANES), i16),
                vmem((units, 2, 2, quarter, LANES), bf16),
                vmem((units, 2, 2, quarter // 2, LANES), i16),
                vmem((units, 2, quarter, LANES), bf16),
                vmem((units, 2, quarter // 2, LANES), i16),
                vmem((units, 2, quarter, LANES), bf16),
                vmem((units, 2, quarter // 2, LANES), i16),
                vmem((units, TOKENS, LANES), f32),
                vmem((LANES, LANES), f32),
                vmem((CHUNKS * TOKENS, LANES), f32),
                vmem((TOKENS, CHUNKS * TOKENS), f32),
                vmem((2, TOKENS, LANES), f32),
                vmem((2, TOKENS, LANES), f32),
                dma((2,)),
                dma,
                dma,
                dma((2, CHUNKS, 2)),
                dma((2, CHUNKS, 2)),
                dma((units, 2, 2, 2)),
                dma((units, 2, 2, 2)),
                dma((units, 2, 2)),
                dma((units, 2, 2)),
                dma((2,)),
                dma((2,)),
            ],
            compiler_params=pltpu.CompilerParams(
                collective_id=0,
                has_side_effects=True,
                vmem_limit_bytes=60 * 1024 * 1024,
            ),
        )(
            tile_live,
            hidden.reshape(PARTS, CHUNKS, piece, width),
            cotangent.reshape(PARTS, CHUNKS, piece, cotan_width),
        )
        return jnp.transpose(sums[:, :, :samples], (1, 0, 2))[None]

    return jax.shard_map(
        per_device,
        mesh=mesh,
        in_specs=placed,
        out_specs=P(("row", "col"), None, "tensor", None),
        check_vma=False,
    )
```
